128 devices in a mesh: req: 32 (over y, z, core), seq: 4 (over x).
Axes of the slice: x: 4, y: 4, z: 4, core: 2. Of those that a mesh axis runs over, the one named last changes fastest.
Arguments:
- hidden_in: bfloat16 [32, 1024, 1792], P('req', 'seq'), may hold values from -6 to 6
- lengths: int32 [32], P('req'), may hold values from 1 to 1024, 16384 in all
- log_decay: float32 [32, 1024, 8], P('req', 'seq'), may hold values from -1 to 0
- mix_gain: float32 [1792], replicated, may hold values from 0.1 to 1.9
- conv_weight: float32 [3, 1792], replicated, may hold values from -3 to 3
- query_weight: bfloat16 [1792, 128], replicated, may hold values from -0.375 to 0.375
- key_weight: bfloat16 [1792, 128], replicated, may hold values from -0.375 to 0.375
- value_weight: bfloat16 [1792, 896], replicated, may hold values from -0.125 to 0.125
- out_weight: bfloat16 [896, 1792], replicated, may hold values from -0.1875 to 0.1875
- mlp_gain: float32 [1792], replicated, may hold values from 0.1 to 1.9
- gate_weight: bfloat16 [1792, 1792], P(None, 'req'), may hold values from -0.125 to 0.125
- up_weight: bfloat16 [1792, 1792], P(None, 'req'), may hold values from -0.125 to 0.125
- down_weight: bfloat16 [1792, 1792], P(None, 'req'), may hold values from -0.125 to 0.125
Outputs:
- layer_out: bfloat16 [32, 1024, 1792], P('req', 'seq')
- end_states: float32 [32, 4, 273, 896], P('req', 'seq')
- end_norms: float32 [32, 4, 273, 8], P('req', 'seq')
The draws below stay inside these ranges and needn't reach their ends.
Inputs may be any that keep to these rules, and one draw needn't show every extreme that they name: Each prompt has at least one token; the lengths sum to 16384 and the longest fills all 1024 slots.
All inputs are finite; a program needn't handle non-finite values. No bound on the sum of `lengths` on one device may be relied on, other than what follows from the above.
Results may differ from the reference program's by a relative error of at most 0.0085.
Values may be sent and summed in bfloat16 or wider, within the bound.
A program may use at most 128 MiB of HBM per device.

```python
import math
import jax
import jax.numpy as jnp
import numpy as np
from jax import lax

D = 1792
HALF_HEADS = 8
DV = 112
FEAT_IN = 16
FF = 1792
KCONV = 3
LOCAL_LEN = 256
REQUEST_COUNT = 32
PROMPT_SLOTS = 1024
TOTAL = 16384
N_SEQ = 4


def draw_log_decay(key, part):
    base_key = jax.random.fold_in(key, 11)
    key_vectors = jax.random.split(base_key, 7)
    share = 0.5
    fast_heads = jax.random.uniform(key_vectors[0], (REQUEST_COUNT, 1, HALF_HEADS)) < share
    fast_rate = jnp.exp(jax.random.uniform(key_vectors[1], (REQUEST_COUNT, 1, HALF_HEADS), jnp.float32, math.log(1.0 / 50.0), math.log(1.0 / 30.0)))
    slow_rate = jnp.exp(jax.random.uniform(key_vectors[2], (REQUEST_COUNT, 1, HALF_HEADS), jnp.float32, math.log(0.1 / PROMPT_SLOTS), math.log(0.6 / PROMPT_SLOTS)))
    base_rate = jnp.where(fast_heads, fast_rate, slow_rate)
    span_factor = jnp.exp(jax.random.uniform(key_vectors[3], (REQUEST_COUNT, PROMPT_SLOTS // LOCAL_LEN, 1, HALF_HEADS), jnp.float32, -0.7, 0.7))
    span_factor = jnp.broadcast_to(span_factor, (REQUEST_COUNT, PROMPT_SLOTS // LOCAL_LEN, LOCAL_LEN, HALF_HEADS)).reshape(REQUEST_COUNT, PROMPT_SLOTS, HALF_HEADS)
    jitter = jnp.exp(jax.random.uniform(key_vectors[4], (REQUEST_COUNT, PROMPT_SLOTS, HALF_HEADS), jnp.float32, -0.7, 0.7))
    spike_position = jax.random.randint(key_vectors[5], (REQUEST_COUNT, 2), 0, PROMPT_SLOTS)
    token_positions = jnp.arange(PROMPT_SLOTS, dtype=jnp.int32)
    spike_flag = jnp.any(token_positions[None, :, None] == spike_position[:, None, :], axis=-1)
    spike_penalty = jax.random.uniform(key_vectors[6], (REQUEST_COUNT, PROMPT_SLOTS, HALF_HEADS), jnp.float32, math.log(0.5), math.log(0.8))
    decay_rates = base_rate * span_factor * jitter
    return (jnp.where(spike_flag[:, :, None], spike_penalty, 0.0) - decay_rates).astype(jnp.float32)


def block_levels(rng, dims, cuts, smallest, high):
    def one(axis_at, shards_of):
        heights = jax.random.uniform(jax.random.fold_in(jax.random.fold_in(rng, 6), axis_at), (shards_of,), jnp.float32, smallest / len(cuts), high / len(cuts))
        return jnp.repeat(jnp.exp(heights), dims[axis_at] // shards_of).reshape((-1,) + (1,) * (len(dims) - axis_at - 1))

    level = one(*cuts[0])
    for cut in cuts[1:]:
        level = level * one(*cut)
    return level


def split_up(count, total, bound, slope):
    loads = [(1 << 20) // math.isqrt(standing ** slope) + 1 for standing in range(2, count + 1)]
    surplus, given = total - bound - (count - 1), [1] * (count - 1)
    while surplus > 0:
        movable = [i for i in range(count - 1) if given[i] < bound]
        pool, left = sum([loads[i] for i in movable]), surplus
        for i in movable:
            extra = min(bound - given[i], max(1, left * loads[i] // pool), surplus)
            given[i] = given[i] + extra
            surplus = surplus - extra
    return np.array([bound] + given)


def ragged_sizes(own_key, amount, total, most, lean):
    if amount == 2:
        one = jax.random.randint(own_key, (), max(1, total - most), min(most, total - 1) + 1)
        return jnp.stack([one, total - one])
    sizes = jnp.asarray(split_up(amount, total, most, lean), jnp.int32)
    couples = (amount - 1) // 2
    source_of, sink = sizes[1:1 + 2 * couples:2], sizes[2:2 + 2 * couples:2]
    margin = jnp.minimum(source_of - 1, most - sink)
    moved = jax.random.randint(jax.random.fold_in(own_key, 1), (couples,), 0, 1 << 20) % (margin + 1)
    sizes = sizes.at[1:1 + 2 * couples:2].set(source_of - moved).at[2:2 + 2 * couples:2].set(sink + moved)
    return sizes[jax.random.permutation(jax.random.fold_in(own_key, 2), amount)]


def noise(key, dims, spread, reach, cuts=(), kind=jnp.bfloat16):
    level = block_levels(key, dims, cuts, -0.22, 0.18) if cuts else 1.0
    entries = jax.random.normal(key, dims, jnp.float32) * spread * level
    return jnp.minimum(jnp.maximum(entries, -reach), reach).astype(kind)


def setup_inputs(seed: int = 0) -> dict:
    keys = jax.random.split(jax.random.key(seed), 14)
    hidden_in = noise(keys[0], (REQUEST_COUNT, PROMPT_SLOTS, D), 1.0, 6.0, ((0, 32), (1, 4)))
    lengths = ragged_sizes(keys[1], REQUEST_COUNT, TOTAL, PROMPT_SLOTS, 2).astype(jnp.int32)
    log_decay = draw_log_decay(jax.random.fold_in(keys[13], 71), 0)
    mix_gain = jnp.clip(1.0 + 0.18 * jax.random.normal(keys[3], (D,), jnp.float32), 0.1, 1.9)
    conv_weight = noise(keys[4], (KCONV, D), 0.6, 3.0, (), jnp.float32)
    query_weight = noise(keys[5], (D, HALF_HEADS * FEAT_IN), (D // 8) ** -0.5, 0.375)
    key_weight = noise(keys[6], (D, HALF_HEADS * FEAT_IN), (D // 8) ** -0.5, 0.375)
    value_weight = noise(keys[7], (D, HALF_HEADS * DV), D ** -0.5, 0.125)
    out_weight = noise(keys[8], (HALF_HEADS * DV, D), (HALF_HEADS * DV) ** -0.5, 0.1875)
    mlp_gain = jnp.clip(1.0 + 0.18 * jax.random.normal(keys[9], (D,), jnp.float32), 0.1, 1.9)
    gate_weight = noise(keys[10], (D, FF), D ** -0.5, 0.125, ((1, 32),))
    up_weight = noise(keys[11], (D, FF), D ** -0.5, 0.125, ((1, 32),))
    down_weight = noise(keys[12], (D, FF), FF ** -0.5, 0.125, ((1, 32),))
    return dict(hidden_in=hidden_in, lengths=lengths, log_decay=log_decay, mix_gain=mix_gain, conv_weight=conv_weight, query_weight=query_weight, key_weight=key_weight, value_weight=value_weight, out_weight=out_weight, mlp_gain=mlp_gain, gate_weight=gate_weight, up_weight=up_weight, down_weight=down_weight)


def features(vectors):
    constant = jnp.ones(vectors.shape[:-1] + (1,), jnp.float32)
    width = vectors.shape[-1]
    squares = (vectors[..., :, None] * vectors[..., None, :]).reshape(vectors.shape[:-1] + (width * width,))
    return jnp.concatenate([constant, vectors, squares * 0.5 ** 0.5], axis=-1)

def block_step(carry, inputs):
    memory, key_sum = carry
    query_blk, key_blk, value_blk, decay_rate, valid_mask = inputs
    highest = lax.Precision.HIGHEST
    cumulative = jnp.cumsum(decay_rate, axis=0)
    scores = jnp.einsum('thi,uhi->htu', query_blk, key_blk, precision=highest)
    kernel = 1.0 + scores + 0.5 * scores * scores
    gap_log = cumulative.T[:, :, None] - cumulative.T[:, None, :]
    block_len = decay_rate.shape[0]
    causal = jnp.arange(block_len)[:, None] >= jnp.arange(block_len)[None, :]
    weights = jnp.where(causal[None], jnp.exp(jnp.minimum(gap_log, 0.0)), 0.0) * kernel * valid_mask[None, None, :]
    rounded = lax.optimization_barrier(weights.astype(jnp.bfloat16))
    numerator = jnp.einsum('htu,uhv->thv', rounded.astype(jnp.float32), value_blk, precision=highest)
    denominator = lax.optimization_barrier(jnp.sum(weights, axis=2)).T
    query_feat = features(query_blk)
    key_feat = features(key_blk) * valid_mask[:, None, None]
    growth = jnp.exp(cumulative)
    numerator = numerator + jnp.einsum('thf,fhv->thv', query_feat, memory, precision=highest) * growth[:, :, None]
    denominator = denominator + jnp.einsum('thf,fh->th', query_feat, key_sum, precision=highest) * growth
    closing = cumulative[-1]
    fading = jnp.exp(closing[None, :] - cumulative)
    faded_keys = key_feat * fading[:, :, None]
    memory = memory * jnp.exp(closing)[None, :, None] + jnp.einsum('uhf,uhv->fhv', faded_keys, value_blk, precision=highest)
    key_sum = key_sum * jnp.exp(closing)[None, :] + lax.optimization_barrier(jnp.sum(faded_keys, axis=0)).T
    return ((memory, key_sum), (numerator, denominator))

def span_attention(query_f32, key_f32, value_f32, decay_rate, valid_mask, memory, key_sum, block_len):
    span = query_f32.shape[0]
    blocks = span // block_len

    def split(array):
        return array.reshape((blocks, block_len) + array.shape[1:])
    carry, outputs = lax.scan(block_step, (memory, key_sum), (split(query_f32), split(key_f32), split(value_f32), split(decay_rate), split(valid_mask)))
    numerator = outputs[0].reshape((span,) + outputs[0].shape[2:])
    denominator = outputs[1].reshape((span,) + outputs[1].shape[2:])
    return (carry[0], carry[1], numerator, denominator)

def rms_scale(rows, gain):
    rows_f32 = rows.astype(jnp.float32)
    factor = lax.rsqrt(lax.optimization_barrier(jnp.mean(rows_f32 * rows_f32, axis=-1, keepdims=True)) + 1e-05)
    return (rows_f32 * factor * gain).astype(jnp.bfloat16)

def reference(hidden_in, lengths, log_decay, mix_gain, conv_weight, query_weight, key_weight, value_weight, out_weight, mlp_gain, gate_weight, up_weight, down_weight):
    head_count = log_decay.shape[2]
    value_len = value_weight.shape[1] // head_count
    feat_in = query_weight.shape[1] // head_count
    feat_len = 1 + feat_in + feat_in * feat_in
    tap_count = conv_weight.shape[0]
    block_len = min(256, LOCAL_LEN)
    feature_scale = feat_in ** (-0.25)

    def one_request(inputs):
        rows_in, length, decays = inputs
        total_len = rows_in.shape[0]
        token_positions = jnp.arange(total_len, dtype=jnp.int32)
        valid_mask = (token_positions < length).astype(jnp.float32)
        normed = rms_scale(rows_in, mix_gain)
        extended = jnp.concatenate([jnp.zeros((tap_count - 1, normed.shape[1]), jnp.bfloat16), normed], axis=0)
        convolved = jnp.zeros(normed.shape, jnp.float32)
        for tap in range(tap_count):
            convolved = convolved + conv_weight[tap][None, :] * extended[tap_count - 1 - tap:tap_count - 1 - tap + total_len].astype(jnp.float32)
        gated_rows = (convolved * jax.nn.sigmoid(normed.astype(jnp.float32))).astype(jnp.bfloat16)
        queries = (jnp.dot(gated_rows, query_weight, preferred_element_type=jnp.float32) * feature_scale).astype(jnp.bfloat16)
        key_rows = (jnp.dot(gated_rows, key_weight, preferred_element_type=jnp.float32) * feature_scale).astype(jnp.bfloat16)
        values = jnp.dot(gated_rows, value_weight, preferred_element_type=jnp.float32).astype(jnp.bfloat16)
        query_f32 = queries.astype(jnp.float32).reshape(total_len, head_count, feat_in)
        key_f32 = key_rows.astype(jnp.float32).reshape(total_len, head_count, feat_in)
        value_f32 = values.astype(jnp.float32).reshape(total_len, head_count, value_len)
        decay_rate = jnp.where(valid_mask[:, None] > 0, decays, 0.0)
        memory = jnp.zeros((feat_len, head_count, value_len), jnp.float32)
        key_sum = jnp.zeros((feat_len, head_count), jnp.float32)
        numer_parts = []
        denom_parts = []
        state_list = []
        norm_list = []
        for segment in range(N_SEQ):
            low = segment * LOCAL_LEN
            high = low + LOCAL_LEN
            memory, key_sum, numerator, denominator = span_attention(query_f32[low:high], key_f32[low:high], value_f32[low:high], decay_rate[low:high], valid_mask[low:high], memory, key_sum, block_len)
            numer_parts.append(numerator)
            denom_parts.append(denominator)
            state_list.append(memory.reshape(feat_len, head_count * value_len))
            norm_list.append(key_sum)
        numerator = jnp.concatenate(numer_parts, axis=0)
        denominator = jnp.concatenate(denom_parts, axis=0)
        attended = (numerator / denominator[:, :, None]).reshape(total_len, head_count * value_len).astype(jnp.bfloat16)
        mixed_rows = (rows_in.astype(jnp.float32) + jnp.dot(attended, out_weight, preferred_element_type=jnp.float32)).astype(jnp.bfloat16)
        mlp_in = rms_scale(mixed_rows, mlp_gain)
        gate_act = jnp.dot(mlp_in, gate_weight, preferred_element_type=jnp.float32)
        up_act = jnp.dot(mlp_in, up_weight, preferred_element_type=jnp.float32)
        hidden_units = (jax.nn.silu(gate_act) * up_act).astype(jnp.bfloat16)
        ffn_out = lax.dot_general(hidden_units, down_weight, (((1,), (1,)), ((), ())), preferred_element_type=jnp.float32)
        result = ((mixed_rows.astype(jnp.float32) + ffn_out) * valid_mask[:, None]).astype(jnp.bfloat16)
        return (result, jnp.stack(state_list), jnp.stack(norm_list))
    layer_out, end_states, end_norms = lax.map(one_request, (hidden_in, lengths, log_decay))
    return (layer_out, end_states, end_norms)
```

```python
import functools

import jax
import jax.numpy as jnp
import numpy as np
from jax import lax
from jax.experimental import pallas as pl
from jax.experimental.pallas import tpu as pltpu
from jax.sharding import PartitionSpec as P

MESH = pl.DeviceIdType.MESH
F32, BF16 = jnp.float32, jnp.bfloat16
D, HEADS, DV, FI, L, SH = 1792, 8, 112, 16, 256, 56
ROWS = 3 * SH + 8
NF = 160
HALF = D // 2
CUT = 96
GROUPS = 4
PER = HEADS // GROUPS


def expansion():
    e = np.zeros((1 + FI + FI * FI, NF), np.float32)
    e[0, 136] = 1
    for i in range(FI):
        e[1 + i, 144 + i] = 1
        for j in range(FI):
            a, d = i, (j - i) % FI
            if d > 8 or (d == 8 and i >= 8):
                a, d = j, (i - j) % FI
            e[17 + FI * i + j, 16 * d + a] = 1
    return e


def nt(a, b):
    return lax.dot_general(a, b, (((1,), (1,)), ((), ())), preferred_element_type=F32)


def nn(a, b):
    return jnp.dot(a, b, preferred_element_type=F32)


def rms(rows, gain):
    factor = lax.rsqrt(jnp.mean(rows * rows, axis=-1, keepdims=True) + 1e-05)
    return (rows * factor * gain).astype(BF16)


def kernel(
    h_ref, len_ref, ld_ref, mg_ref, cw_ref, wq_hbm, wk_hbm, wv_hbm, wo_hbm, pg_ref,
    g_ref, u_ref, d_ref, e_ref,
    out_ref, st_ref, nm_ref,
    G, wq, wk, wv, wo, halo, nbuf, gbuf, kn, qt, kt, vt, near, phiq, mloc, prior, msend,
    att, mt, ntr, cumt, cumn, fade, grow, mixed, mlp, acc,
    load_sem, send_sem, recv_sem, psend, precv, hsem, csend, crecv,
):
    req, seq = lax.axis_index("req"), lax.axis_index("seq")
    y, z, c = req // 8, (req // 2) % 4, req % 2

    def at(yy, zz, cc):
        return (yy * 4 + zz) * 2 + cc

    def near_z(k):
        return at(y, (z + k + 4) % 4, c)

    def near_y(k):
        return at((y + k + 4) % 4, z, c)

    partner = at(y, z, 1 - c)
    loads = [
        pltpu.make_async_copy(src, dst, load_sem.at[i])
        for i, (src, dst) in enumerate(((wq_hbm, wq), (wk_hbm, wk), (wv_hbm, wv), (wo_hbm, wo)))
    ]
    for load in loads:
        load.start()

    barrier = pltpu.get_barrier_semaphore()
    for r, s in (
        (near_z(1), seq), (near_z(-1), seq), (near_y(1), seq), (near_y(-1), seq),
        (partner, seq), (req, (seq + 1) % 4), (req, (seq + 3) % 4),
    ):
        pl.semaphore_signal(barrier, inc=1, device_id=(r, s), device_id_type=MESH)

    @pl.loop(0, 7)
    def _(j):
        cols = pl.ds(pl.multiple_of(j * 256, 256), 256)
        parts = [ref[:, cols].astype(F32) for ref in (g_ref, u_ref, d_ref)]
        parts.append(jnp.zeros((8, 256), F32))
        G[req, :, cols] = jnp.concatenate(parts, axis=0).astype(BF16)

    @pl.when(seq == 0)
    def _():
        prior[...] = jnp.zeros_like(prior)

    pl.semaphore_wait(barrier, 7)

    halo_copy = pltpu.make_async_remote_copy(
        h_ref.at[pl.ds(L - 16, 16)], halo, hsem.at[0], hsem.at[1],
        device_id=(req, (seq + 1) % 4), device_id_type=MESH,
    )

    @pl.when(seq < 3)
    def _():
        halo_copy.start()

    count = [0]
    started, waiting = [], {}

    def shard(part, a1, a2):
        yy, zz = (a2, a1) if part == 0 else (a1, a2)
        return at((y + yy + 4) % 4, (z + zz + 4) % 4, c)

    def to(part, axis, k):
        along_z = (part == 0) == (axis == 1)
        return near_z(k) if along_z else near_y(k)

    def region(slot, part, piece):
        cols = pl.ds(part * HALF, HALF)
        rows = (pl.ds(0, ROWS), pl.ds(0, CUT), pl.ds(CUT, ROWS - CUT))[piece]
        return G.at[slot, rows, cols]

    def send(key, part, axis, k, slot, piece, slot_in):
        n = count[0]
        count[0] += 1
        src = region(slot, part, piece)
        copy = pltpu.make_async_remote_copy(
            src, src, send_sem.at[n], recv_sem.at[n],
            device_id=(to(part, axis, k), seq), device_id_type=MESH,
        )
        copy.start()
        started.append(copy)
        dst = region(slot_in, part, piece)
        waiting[key] = pltpu.make_async_remote_copy(
            dst, dst, send_sem.at[n], recv_sem.at[n],
            device_id=(to(part, axis, k), seq), device_id_type=MESH,
        )

    pcount = [0]
    pwaiting = {}

    def other(slot):
        return slot + 1 - 2 * c

    def share(key, part, slot):
        n = pcount[0]
        pcount[0] += 1
        src, dst = region(slot, part, 0), region(other(slot), part, 0)
        copy = pltpu.make_async_remote_copy(
            src, src, psend.at[n], precv.at[n], device_id=(partner, seq), device_id_type=MESH
        )
        copy.start()
        started.append(copy)
        pwaiting[key] = pltpu.make_async_remote_copy(
            dst, dst, psend.at[n], precv.at[n], device_id=(partner, seq), device_id_type=MESH
        )

    OFF = (0, -1, 1, 2)

    def first(part):
        for k in (1, -1):
            send(("p1", part, k), part, 1, k, shard(part, 0, 0), 0, shard(part, -k, 0))

    def second(part, j):
        a1 = OFF[j]
        for k in (1, -1):
            send(("q1", part, j, k), part, 2, k, shard(part, a1, 0), 0, shard(part, a1, -k))

    def forward_first(part):
        for k in (1, -1):
            waiting[("p1", part, k)].wait_recv()
            piece = 1 if k == 1 else 2
            send(("p2", part, k), part, 1, k, shard(part, -k, 0), piece, shard(part, 2, 0))

    def forward_second(part, j):
        a1 = OFF[j]
        for k in (1, -1):
            waiting[("q1", part, j, k)].wait_recv()
            piece = 2 if k == 1 else 1
            send(("q2", part, j, k), part, 2, k, shard(part, a1, -k), piece, shard(part, a1, 2))
        for k in (1, -1):
            share((part, a1, -k), part, shard(part, a1, -k))

    def finish_second(part, j):
        for k in (1, -1):
            waiting[("q2", part, j, k)].wait_recv()
        share((part, OFF[j], 2), part, shard(part, OFF[j], 2))

    def service(point):
        both = (0, 1)
        if point == 0:
            for part in both:
                first(part)
            for part in both:
                second(part, 0)
            for part in both:
                share((part, 0, 0), part, shard(part, 0, 0))
        if point == 1:
            for part in both:
                forward_first(part)
            for j in (1, 2):
                for part in both:
                    second(part, j)
            for part in both:
                for k in (1, -1):
                    share((part, -k, 0), part, shard(part, -k, 0))
        if point == 2:
            for part in both:
                for k in (1, -1):
                    waiting[("p2", part, k)].wait_recv()
                second(part, 3)
                share((part, 2, 0), part, shard(part, 2, 0))
            for part in both:
                forward_second(part, 0)
        if point == 3:
            for j in (1, 2):
                for part in both:
                    forward_second(part, j)
        if point == 4:
            for part in both:
                forward_second(part, 3)
            for part in both:
                finish_second(part, 0)
        if point == 5:
            for j in (1, 2):
                for part in both:
                    finish_second(part, j)
        if point == 6:
            for part in both:
                finish_second(part, 3)

    def arrived(*keys):
        for dy, dz in keys:
            pwaiting[(0, dz, dy)].wait_recv()
            pwaiting[(1, dy, dz)].wait_recv()

    service(0)

    @pl.loop(0, 8)
    def _(b):
        rows = pl.ds(pl.multiple_of(b * 32, 32), 32)
        block = rms(h_ref[rows, :].astype(F32), mg_ref[...])
        nbuf[pl.ds(pl.multiple_of(b * 32 + 8, 8), 32), :] = block.astype(F32)

    length = len_ref[0] - seq * L
    valid_row = lax.broadcasted_iota(jnp.int32, (1, L), 1) < length
    valid_col = lax.broadcasted_iota(jnp.int32, (L, 1), 0) < length
    rate = jnp.where(valid_row, ld_ref[...], 0.0)
    upper = lax.broadcasted_iota(jnp.int32, (L, L), 0) <= lax.broadcasted_iota(jnp.int32, (L, L), 1)
    cum = jnp.dot(
        rate, upper.astype(F32), precision=lax.Precision.HIGHEST, preferred_element_type=F32
    )
    cumn[...] = cum.T
    closing = cum[:, L - 1 :]
    fades = jnp.where(valid_row, jnp.exp(closing - cum), 0.0)
    grows = jnp.exp(cum)
    for h in range(HEADS):
        cumt[h] = cum[h : h + 1]
        fade[h] = fades[h : h + 1]
        grow[h] = grows[h : h + 1]

    @pl.when(seq == 0)
    def _():
        nbuf[pl.ds(0, 8), :] = jnp.zeros((8, D), F32)

    @pl.when(seq > 0)
    def _():
        halo_copy.wait_recv()
        block = rms(halo[...].astype(F32), mg_ref[...]).astype(F32)
        nbuf[pl.ds(0, 8), :] = block[8:16]

    @pl.loop(0, 8)
    def _(b):
        rows = pl.ds(pl.multiple_of(b * 32, 32), 32)
        block = nbuf[pl.ds(pl.multiple_of(b * 32, 8), 40), :]
        here = block[8:40]
        conv = cw_ref[0:1] * here + cw_ref[1:2] * block[7:39] + cw_ref[2:3] * block[6:38]
        gbuf[rows, :] = (conv * jax.nn.sigmoid(here)).astype(BF16)

    loads[0].wait()
    loads[1].wait()
    qn = (nn(gbuf[...], wq[...]) * 0.5).astype(BF16)
    keys = (nn(gbuf[...], wk[...]) * 0.5).astype(BF16)
    kn[...] = keys
    qt[...] = qn.astype(F32).T
    kt[...] = keys.astype(F32).T
    loads[2].wait()

    @pl.loop(0, 2)
    def _(b):
        rows = pl.ds(pl.multiple_of(b * 128, 128), 128)
        values = nn(gbuf[rows, :], wv[...])
        turned = values.T.astype(BF16)
        for h in range(HEADS):
            vt[h, 0:DV, rows] = turned[h * DV : (h + 1) * DV]

    ones = (lax.broadcasted_iota(jnp.int32, (16, L), 0) == 0).astype(BF16)
    for h in range(HEADS):
        vt[h, DV:128, :] = ones

    service(1)

    row16 = lax.broadcasted_iota(jnp.int32, (16, L), 0)
    lane128 = lax.broadcasted_iota(jnp.int32, (L, 128), 1)

    def phi(x, w, middle, square):
        parts = [x * w * square]
        for d in range(1, 9):
            parts.append(w * pltpu.roll(x, 16 - d, 0))
        parts[0] = square * (w * x)
        parts[8] = jnp.where(row16 < 8, parts[8], jnp.where(row16 == 8, middle, 0.0))
        parts.append(w)
        return jnp.concatenate(parts, axis=0).astype(BF16)

    @pl.loop(0, HEADS)
    def _(h):
        head = pl.ds(pl.multiple_of(h * 16, 16), 16)
        k_h, q_h = kt[head, :], qt[head, :]
        k_only = jnp.where(lane128 // 16 == h, kn[...], jnp.zeros_like(kn))
        scores = nn(k_only, qt[...].astype(BF16))
        lane8 = lax.broadcasted_iota(jnp.int32, (L, HEADS), 1)
        col = jnp.sum(jnp.where(lane8 == h, cumn[...], 0.0), axis=1, keepdims=True)
        gap = jnp.minimum(cumt[h] - col, 0.0)
        causal = lax.broadcasted_iota(jnp.int32, (L, L), 0) <= lax.broadcasted_iota(
            jnp.int32, (L, L), 1
        )
        weights = jnp.where(causal, jnp.exp(gap), 0.0) * ((0.5 * scores + 1.0) * scores + 1.0)
        near[h] = nn(vt[h], weights.astype(BF16))
        f_h, g_h = fade[h], grow[h]
        mloc[h] = nt(phi(k_h, k_h * f_h, jnp.broadcast_to(f_h, (16, L)), 1.0), vt[h])
        phiq[h] = phi(q_h, q_h * g_h, jnp.broadcast_to(g_h, (16, L)), 0.5)

    service(2)

    for g in range(GROUPS):
        heads = pl.ds(g * PER, PER)
        chain = pltpu.make_async_remote_copy(
            msend.at[heads], prior.at[heads], csend.at[g], crecv.at[g],
            device_id=(req, (seq + 1) % 4), device_id_type=MESH,
        )

        @pl.when(seq > 0)
        def _():
            chain.wait_recv()

        for h in range(g * PER, (g + 1) * PER):
            end = prior[h].astype(F32) * grow[h][:, L - 1 :] + mloc[h]
            mloc[h] = end
            msend[h] = end.astype(BF16)

        @pl.when(seq < 3)
        def _():
            chain.start()

    @pl.loop(0, HEADS)
    def _(h):
        before = prior[h].astype(F32).T.astype(BF16)
        numer = near[h] + nn(before, phiq[h])
        rows = pl.ds(pl.multiple_of(h * DV, 16), DV)
        att[rows, :] = (numer[0:DV] / numer[DV : DV + 1]).astype(BF16)
        turned = mloc[h].T
        mt[rows, :] = turned[0:DV]
        ntr[pl.ds(h, 1), :] = turned[DV : DV + 1]

    loads[3].wait()
    attended = att[...].astype(F32).T.astype(BF16)
    mixed[...] = (h_ref[...].astype(F32) + nn(attended, wo[...])).astype(BF16)

    @pl.loop(0, 8)
    def _(b):
        rows = pl.ds(pl.multiple_of(b * 32, 32), 32)
        mlp[rows, :] = rms(mixed[rows, :].astype(F32), pg_ref[...])

    service(3)

    def pair(first_chip, second_chip, start=False):
        bases = [at((y + dy + 4) % 4, (z + dz + 4) % 4, 0) for dy, dz in (first_chip, second_chip)]
        turned = []
        for base in bases:
            weights = G[pl.ds(base, 2), 0 : 2 * SH, :].reshape(4 * SH, D)
            both = nt(weights, mlp[...])
            for s in range(2):
                gate = both[s * 2 * SH : s * 2 * SH + SH]
                up = both[s * 2 * SH + SH : (s + 1) * 2 * SH]
                turned += [jax.nn.silu(gate) * up, jnp.zeros((8, L), F32)]
        hidden = jnp.concatenate(turned, axis=0).T.astype(BF16)
        total = nn(hidden[:, 0:128], G[pl.ds(bases[0], 2), 2 * SH : ROWS, :].reshape(128, D))
        total += nn(hidden[:, 128:256], G[pl.ds(bases[1], 2), 2 * SH : ROWS, :].reshape(128, D))
        acc[...] = total if start else acc[...] + total

    arrived((0, 0), (0, 1), (0, -1), (1, 0), (-1, 0))
    pair((0, 1), (0, -1), start=True)
    pair((1, 0), (-1, 0))

    e = e_ref[...]
    states = mt[...]
    high = states.astype(BF16)
    low = (states - high.astype(F32)).astype(BF16)
    row = lax.broadcasted_iota(jnp.int32, (273, 1), 0)
    scale = jnp.where(row < 17, 1.0, 0.5**0.5)
    st_ref[...] = (nt(e, high) + nt(e, low)) * scale
    sums = ntr[...]
    high = sums.astype(BF16)
    low = (sums - high.astype(F32)).astype(BF16)
    lane = lax.broadcasted_iota(jnp.int32, (1, 273), 1)
    nm_ref[...] = (nt(high, e) + nt(low, e)) * jnp.where(lane < 17, 1.0, 0.5**0.5)

    arrived((1, 1), (1, -1), (-1, 1), (-1, -1))
    pair((1, 1), (1, -1))
    pair((-1, 1), (-1, -1))
    service(4)
    arrived((2, 0), (0, 2))
    pair((2, 0), (0, 2))
    service(5)
    arrived((1, 2), (-1, 2), (2, 1), (2, -1))
    pair((1, 2), (-1, 2))
    pair((2, 1), (2, -1))
    service(6)
    arrived((2, 2))
    pair((0, 0), (2, 2))
    out_ref[...] = jnp.where(valid_col, mixed[...].astype(F32) + acc[...], 0.0).astype(BF16)

    for copy in started:
        copy.wait_send()

    @pl.when(seq < 3)
    def _():
        halo_copy.wait_send()
        for g in range(GROUPS):
            heads = pl.ds(g * PER, PER)
            pltpu.make_async_remote_copy(
                msend.at[heads], prior.at[heads], csend.at[g], crecv.at[g],
                device_id=(req, (seq + 1) % 4), device_id_type=MESH,
            ).wait_send()


def local(
    hidden_in, lengths, log_decay, mix_gain, conv_weight, query_weight, key_weight, value_weight,
    out_weight, mlp_gain, gate_weight, up_weight, down_weight,
):
    vmem = pl.BlockSpec(memory_space=pltpu.VMEM)
    smem = pl.BlockSpec(memory_space=pltpu.SMEM)
    anywhere = pl.BlockSpec(memory_space=pl.ANY)
    dma = pltpu.SemaphoreType.DMA
    result, states, norms = pl.pallas_call(
        kernel,
        name="layer",
        out_shape=(
            jax.ShapeDtypeStruct((L, D), BF16),
            jax.ShapeDtypeStruct((273, HEADS * DV), F32),
            jax.ShapeDtypeStruct((HEADS, 273), F32),
        ),
        in_specs=[vmem, smem, vmem, vmem, vmem] + [anywhere] * 4 + [vmem] * 5,
        out_specs=(vmem, vmem, vmem),
        scratch_shapes=[
            pltpu.VMEM((32, ROWS, D), BF16),
            pltpu.VMEM((D, 128), BF16),
            pltpu.VMEM((D, 128), BF16),
            pltpu.VMEM((D, HEADS * DV), BF16),
            pltpu.VMEM((HEADS * DV, D), BF16),
            pltpu.VMEM((16, D), BF16),
            pltpu.VMEM((L + 8, D), F32),
            pltpu.VMEM((L, D), BF16),
            pltpu.VMEM((L, 128), BF16),
            pltpu.VMEM((128, L), F32),
            pltpu.VMEM((128, L), F32),
            pltpu.VMEM((HEADS, 128, L), BF16),
            pltpu.VMEM((HEADS, 128, L), F32),
            pltpu.VMEM((HEADS, NF, L), BF16),
            pltpu.VMEM((HEADS, NF, 128), F32),
            pltpu.VMEM((HEADS, NF, 128), BF16),
            pltpu.VMEM((HEADS, NF, 128), BF16),
            pltpu.VMEM((HEADS * DV, L), BF16),
            pltpu.VMEM((HEADS * DV, NF), F32),
            pltpu.VMEM((HEADS, NF), F32),
            pltpu.VMEM((HEADS, 1, L), F32),
            pltpu.VMEM((L, HEADS), F32),
            pltpu.VMEM((HEADS, 1, L), F32),
            pltpu.VMEM((HEADS, 1, L), F32),
            pltpu.VMEM((L, D), BF16),
            pltpu.VMEM((L, D), BF16),
            pltpu.VMEM((L, D), F32),
            dma((4,)),
            dma((40,)),
            dma((40,)),
            dma((32,)),
            dma((32,)),
            dma((2,)),
            dma((GROUPS,)),
            dma((GROUPS,)),
        ],
        compiler_params=pltpu.CompilerParams(
            collective_id=0, has_side_effects=True, vmem_limit_bytes=63 * 1024 * 1024
        ),
    )(
        hidden_in[0], lengths, log_decay[0].T, mix_gain[None], conv_weight, query_weight,
        key_weight, value_weight, out_weight, mlp_gain[None], gate_weight.T, up_weight.T,
        down_weight.T, jnp.asarray(expansion(), BF16),
    )
    return (result[None], states[None, None], norms.T[None, None])


def solution(mesh):
    return jax.shard_map(
        local,
        mesh=mesh,
        in_specs=(
            P("req", "seq", None),
            P("req"),
            P("req", "seq", None),
            P(),
            P(),
            P(),
            P(),
            P(),
            P(),
            P(),
            P(None, "req"),
            P(None, "req"),
            P(None, "req"),
        ),
        out_specs=(P("req", "seq", None), P("req", "seq", None, None), P("req", "seq", None, None)),
        check_vma=False,
    )
```
